32 devices in a mesh: grp: 2 (over y), occ: 4 (over z), aux: 4 (over x, core).
Axes of the slice: x: 2, y: 2, z: 4, core: 2. Of those that a mesh axis runs over, the one named last changes fastest.
Arguments:
- factors: float32 [8192, 3072], P(('grp', 'aux'), 'occ'), parts along dimension 0, may hold values from -0.75 to 0.75
- eps_occ: float32 [32], P('grp'), parts along dimension 0, may hold values from -2 to -0.5
- eps_vir: float32 [6144], P('grp'), parts along dimension 0, may hold values from 0.2 to 3
- tile_index: int32 [2], P('grp'), parts along dimension 0, may hold values from 0 to 15
- pair_offset: int32 [2], P('grp'), parts along dimension 0, may hold values from 1 to 3
Outputs:
- gradient: float32 [8192, 3072], P(('grp', 'aux'), 'occ'), parts along dimension 0
The draws below stay inside these ranges and needn't reach their ends.
There are 2 independent parts, one for each index of `grp`. The reference program is written for one: setup_inputs(seed, part) draws one part's arguments, and reference() takes and returns one part's arrays. A program takes and returns all parts, laid end to end along the dimension named above; each array names one. Nothing has to cross between parts.
All inputs are finite; a program needn't handle non-finite values.
Results may differ from the reference program's by a relative error of at most 0.0001.
Values sent between devices are 32-bit elements; how exact they have to be, the bound alone decides.
A program may use at most 64 MiB of HBM per device.

```python
import jax
import jax.numpy as jnp
from jax import lax

NAUX = 4096
VT = 192
NVIRT = 3072
BLK = 4
DMAX = 3
STEPS = 1
OCC = 16


def shard_levels(rng, dims, split, least, high):
    level = 1.0
    for position, blocks in split:
        steps = jax.random.uniform(jax.random.fold_in(jax.random.fold_in(rng, 6), position), (blocks,), jnp.float32, least / len(split), high / len(split))
        level = level * jnp.repeat(jnp.exp(steps), dims[position] // blocks).reshape((-1,) + (1,) * (len(dims) - 1 - position))
    return level


def bell_draw(key, shape, scale, bound, shards=(), kind=jnp.bfloat16):
    factor_of = shard_levels(key, shape, shards, -0.22, 0.18) if shards else 1.0
    entries = jax.random.normal(key, shape, jnp.float32) * scale * factor_of
    return jnp.minimum(jnp.maximum(entries, -bound), bound).astype(kind)


def setup_inputs(seed: int = 0, part: int = 0) -> dict:
    arg_keys = jax.random.split(jax.random.key(seed), 6)
    part_keys = jax.random.split(jax.random.fold_in(arg_keys[5], part), 6)
    factors = bell_draw(part_keys[0], (NAUX, OCC * VT), 0.125, 0.75, ((0, 4), (1, 4)), jnp.float32)
    eps_occ = jnp.clip(jax.random.uniform(part_keys[1], (OCC,), jnp.float32, -2.0, -0.5), -2.0, -0.5)
    eps_vir = jnp.clip(jax.random.uniform(part_keys[2], (NVIRT,), jnp.float32, 0.2, 3.0), 0.2, 3.0)
    tile_index = jax.random.randint(part_keys[3], (1,), 0, NVIRT // VT).astype(jnp.int32)
    pair_offset = jax.random.randint(part_keys[4], (STEPS,), 1, DMAX + 1).astype(jnp.int32)
    return {"factors": factors, "eps_occ": eps_occ, "eps_vir": eps_vir, "tile_index": tile_index, "pair_offset": pair_offset}


PRECISE = lax.Precision.HIGHEST


def inner_dot(left, right):
    return lax.dot_general(left, right, (((0,), (0,)), ((), ())), precision=PRECISE, preferred_element_type=jnp.float32)


def reference(factors, eps_occ, eps_vir, tile_index, pair_offset):
    tile_width = BLK * VT
    block_count = eps_occ.shape[0] // BLK
    blocks = factors.reshape(NAUX, block_count, tile_width).transpose(1, 0, 2)
    vir_energy = lax.dynamic_slice_in_dim(eps_vir, tile_index[0].astype(jnp.int32) * VT, VT)
    gaps = (vir_energy[None, None, :] - eps_occ.reshape(block_count, BLK)[:, :, None]).reshape(block_count, tile_width)
    gradient = jnp.zeros((block_count, NAUX, tile_width), jnp.float32)
    block_ids = jnp.arange(block_count, dtype=jnp.int32)
    for step_index in range(STEPS):
        partner_ids = ((block_ids - pair_offset[step_index]) % block_count).astype(jnp.int32)

        def pair_terms(block_id):
            partner_id = partner_ids[block_id]
            own_rows = blocks[block_id]
            far_rows = blocks[partner_id]
            pair_ints = inner_dot(own_rows, far_rows)
            amplitude = pair_ints / (gaps[block_id][:, None] + gaps[partner_id][None, :])
            own_grad = jnp.dot(far_rows, amplitude.T, precision=PRECISE, preferred_element_type=jnp.float32)
            far_grad = jnp.dot(own_rows, amplitude, precision=PRECISE, preferred_element_type=jnp.float32)
            return own_grad, far_grad

        own_grad, far_grad = lax.map(pair_terms, block_ids)
        gradient = gradient + own_grad
        gradient = gradient.at[partner_ids].add(far_grad)
    return gradient.transpose(1, 0, 2).reshape(NAUX, block_count * tile_width)
```

```python
import functools

import jax
import jax.numpy as jnp
from jax import lax
from jax.experimental import pallas as pl
from jax.experimental.pallas import tpu as pltpu
from jax.sharding import PartitionSpec as P

VT = 192
BLK = 4
DMAX = 3
WIDTH = 128
PARTS = 8
LAG = 2
LINE = 4
SHARDS = 4
MESH = pl.DeviceIdType.MESH

PRECISE = lax.Precision.HIGH


def inner_dot(left, right):
    return lax.dot_general(
        left, right, (((0,), (0,)), ((), ())), precision=PRECISE, preferred_element_type=jnp.float32
    )


def outer_dot(left, right):
    return lax.dot_general(
        left, right, (((1,), (1,)), ((), ())), precision=PRECISE, preferred_element_type=jnp.float32
    )


def gaps_of(vir_energy, energies):
    return (vir_energy[None, :] - energies[:, None]).reshape(-1)


def amplitude_of(own, far, own_gaps, far_gaps, weight):
    aux_count = lax.axis_size("aux")
    aux_rank = lax.axis_index("aux")
    share = far.shape[1] // aux_count
    ints = lax.psum_scatter(inner_dot(far, own), "aux", scatter_dimension=0, tiled=True)
    gaps = lax.dynamic_slice_in_dim(far_gaps, aux_rank * share, share)
    amplitude = jnp.where(weight > 0, weight * (ints / (gaps[:, None] + own_gaps[None, :])), 0.0)
    return lax.all_gather(amplitude, "aux", axis=0, tiled=True)


def term(far, amplitude):
    return jnp.dot(far, amplitude, precision=PRECISE, preferred_element_type=jnp.float32)


def local_ring(factors, eps_occ, eps_vir, tile_index, pair_offset):
    count = lax.axis_size("occ")
    me = lax.axis_index("occ")
    vir_energy = lax.dynamic_slice_in_dim(eps_vir, tile_index[0] * VT, VT)
    energy = eps_occ.reshape(count, BLK)
    own_gaps = gaps_of(vir_energy, energy[me])
    offset = pair_offset[0]
    total = jnp.zeros_like(factors)
    for sign in (1, -1):
        far = factors
        held = factors
        for hop in range(1, DMAX + 1):
            held = lax.ppermute(held, "occ", [(i, (i + sign) % count) for i in range(count)])
            far = jnp.where(offset == hop, held, far)
        far_gaps = gaps_of(vir_energy, energy[(me - sign * offset) % count])
        total = total + term(far, amplitude_of(factors, far, own_gaps, far_gaps, jnp.float32(1)))
    return total


def split(x):
    high = x.astype(jnp.bfloat16)
    return high, (x - high.astype(jnp.float32)).astype(jnp.bfloat16)


def dot3(left, right, dims):
    dot = functools.partial(lax.dot_general, dimension_numbers=(dims, ((), ())), preferred_element_type=jnp.float32)
    return dot(left[0], right[0]) + (dot(left[0], right[1]) + dot(left[1], right[0]))


def line_kernel(
    aux, own_hbm, occ_hbm, vir_hbm, tile_hbm, offset_hbm, total_out,
    own, right1, left1, right2, left2, res, relay1, relay2, total, own_hi, own_lo, far_hi, far_lo,
    ints, core_in, half, x_in, amp, amp_hi, amp_lo, table, own_row, gap_cols,
    occ_energy, vir_energy, tile, offset,
    r1_s, r1_r, l1_s, l1_r, r2_s, r2_r, l2_s, l2_r,
    a_s, a_r, b_s, b_r, c_s, c_r, own_s, small_s, out_s,
):
    chunks, rows, width = right1.shape
    tile_width = own.shape[1]
    share = width // 2
    band = rows // PARTS
    pair = 2 * band
    me = lax.axis_index("occ")
    rank = lax.axis_index("aux")
    first, last = me == 0, me == LINE - 1
    left, right = {"occ": me - 1}, {"occ": me + 1}
    core = {"aux": rank + 1 - 2 * (rank % 2)}
    xpeer = {"aux": (rank + 2) % aux}
    mine = pl.multiple_of((rank % 2) * share, share)
    theirs = pl.multiple_of((1 - rank % 2) * share, share)

    def remote(src, dst, send, recv, target):
        return pltpu.make_async_remote_copy(
            src_ref=src, dst_ref=dst, send_sem=send, recv_sem=recv, device_id=target, device_id_type=MESH
        )

    def columns(c):
        return pl.ds(pl.multiple_of(c * width, width), width)

    def band_of(t):
        return pl.ds(pl.multiple_of(t * band, band), band)

    def pair_of(u):
        return pl.ds(pl.multiple_of(u * pair, pair), pair)

    def piece(ref, c, t):
        return ref.at[c, band_of(t)]

    def own_piece(c, t):
        return own_hbm.at[band_of(t), columns(c)]

    def r1(src, c, t):
        return remote(src, piece(right1, c, t), r1_s, r1_r.at[c, t], left)

    def l1(src, c, t):
        return remote(src, piece(left1, c, t), l1_s, l1_r.at[c, t], right)

    def r2(src, c, t):
        return remote(src, piece(right2, c, t), r2_s, r2_r.at[c, t], left)

    def l2(src, c, t):
        return remote(src, piece(left2, c, t), l2_s, l2_r.at[c, t], right)

    def got_r1(c, t):
        r1(piece(right1, c, t), c, t).wait_recv()

    def got_l1(c, t):
        l1(piece(left1, c, t), c, t).wait_recv()

    def got_r2(c, t):
        r2(piece(right2, c, t), c, t).wait_recv()

    def got_l2(c, t):
        l2(piece(left2, c, t), c, t).wait_recv()

    def a_copy(i):
        return remote(ints.at[i, pl.ds(theirs, share)], core_in.at[i], a_s, a_r.at[i], core)

    def b_copy(i):
        return remote(half.at[i], x_in.at[i], b_s, b_r.at[i], xpeer)

    def c_copy(i):
        rows_of = amp.at[i, pl.ds(mine, share)]
        return remote(rows_of, rows_of, c_s, c_r.at[i], core)

    def own_copy(t):
        return pltpu.make_async_copy(own_hbm.at[band_of(t)], own.at[band_of(t)], own_s.at[t])

    def small_copies():
        pairs = ((occ_hbm, occ_energy), (vir_hbm, vir_energy), (tile_hbm, tile), (offset_hbm, offset))
        return [pltpu.make_async_copy(src, dst, small_s.at[n]) for n, (src, dst) in enumerate(pairs)]

    def out_copy(c, t):
        at = (band_of(t), columns(c))
        return pltpu.make_async_copy(total.at[at], total_out.at[at], out_s)

    for copy in small_copies():
        copy.start()

    @pl.loop(0, PARTS)
    def _(t):
        own_copy(t).start()

    barrier = pltpu.get_barrier_semaphore()
    for target in (core, xpeer):
        pl.semaphore_signal(barrier, inc=1, device_id=target, device_id_type=MESH)

    @pl.when(me > 0)
    def _():
        pl.semaphore_signal(barrier, inc=1, device_id=left, device_id_type=MESH)

    @pl.when(me < LINE - 1)
    def _():
        pl.semaphore_signal(barrier, inc=1, device_id=right, device_id_type=MESH)

    ends = jnp.logical_or(first, last)

    @pl.when(ends)
    def _():
        pl.semaphore_wait(barrier, 3)

    @pl.when(jnp.logical_not(ends))
    def _():
        pl.semaphore_wait(barrier, 4)

    def send_own(c, t):
        @pl.when(first)
        def _():
            l1(own_piece(c, t), c, t).start()

        @pl.when(jnp.logical_or(me == 1, last))
        def _():
            r1(own_piece(c, t), c, t).start()

    @pl.loop(0, PARTS)
    def _(t):
        send_own(0, t)

    for copy in small_copies():
        copy.wait()

    odd = offset[0] & 1

    def pick(odd_one, even_one):
        return jnp.where(jnp.full(odd_one.shape, odd, jnp.int32) > 0, odd_one, even_one)

    def gap_table():
        tall = (8, width)
        place = lax.broadcasted_iota(jnp.int32, tall, 0) * width + lax.broadcasted_iota(jnp.int32, tall, 1)
        orbital = jnp.zeros(tall, jnp.int32)
        for n in range(1, BLK):
            orbital = orbital + jnp.where(place >= n * VT, 1, 0)
        virtual = place - orbital * VT
        base = tile[0] * VT
        energies = lax.fori_loop(
            0, VT, lambda a, so_far: jnp.where(virtual == a, vir_energy[base + a], so_far), jnp.zeros(tall, jnp.float32)
        )

        def of_block(block):
            value = jnp.zeros(tall, jnp.float32)
            for n in range(BLK):
                value = jnp.where(orbital == n, occ_energy[block * BLK + n], value)
            return value

        odd_block = (me + 1) % LINE
        even_block = jnp.where(first, 1, jnp.where(me == 1, LINE - 1, 0))
        table[0:8, :] = energies - of_block(me)
        table[8:16, :] = energies - pick(of_block(odd_block), of_block(even_block))
        for r in range(chunks):
            own_row[:, r * width : (r + 1) * width] = table[r : r + 1, :]

        @pl.loop(0, chunks)
        def _(i):
            gap_cols[i] = jnp.broadcast_to(table[pl.ds(8 + i, 1), :], (width, width)).T

    def split_far(c, t, far):
        span = band_of(t)
        far_hi[c, span, :], far_lo[c, span, :] = split(far)

    def serve_left(s):
        c, t = s // PARTS, s % PARTS

        @pl.when(jnp.logical_and(s >= 0, c < chunks))
        def _():
            got_l1(c, t)
            l1(piece(left1, c, t), c, t).start()
            span = band_of(t)
            split_far(c, t, pick(right1[c, span, :], left1[c, span, :]))

        @pl.when(c >= chunks)
        def _():
            d = c - chunks
            span = band_of(t)
            got_l2(d, t)
            relay2[d, span, :] = pick(res[d, span, :], left2[d, span, :])
            l2(piece(relay2, d, t), d, t).start()

    def serve(k, t):
        span = band_of(t)

        @pl.when(me == 1)
        def _():
            @pl.when(k < chunks)
            def _():
                got_l1(k, t)
                l1(piece(left1, k, t), k, t).start()

            @pl.when(k >= chunks)
            def _():
                d = k - chunks
                got_r2(d, t)
                r2(piece(right2, d, t), d, t).start()

        @pl.when(me == 2)
        def _():
            @pl.when(k < chunks)
            def _():
                got_r1(k, t)
                relay1[k, span, :] = pick(own[span, columns(k)], right1[k, span, :])
                r1(piece(relay1, k, t), k, t).start()

            @pl.when(k >= chunks)
            def _():
                d = k - chunks
                got_r2(d, t)
                right2[d, span, :] = pick(right2[d, span, :], res[d, span, :])
                r2(piece(right2, d, t), d, t).start()

            serve_left(k * PARTS + t - LAG)

    def arrive(k, t):
        c = k - 1
        span = band_of(t)

        @pl.when(jnp.logical_and(k >= 1, k <= chunks))
        def _():
            @pl.when(me < 2)
            def _():
                got_r1(c, t)
                split_far(c, t, right1[c, span, :])

            @pl.when(last)
            def _():
                got_l1(c, t)
                split_far(c, t, left1[c, span, :])

        @pl.when(k + 1 < chunks)
        def _():
            send_own(k + 1, t)

    def finish(c, t):
        span = band_of(t)
        at = (span, columns(c))

        @pl.when(first)
        def _():
            got_r2(c, t)
            total[at] += right2[c, span, :]

        @pl.when(jnp.logical_or(me == 1, last))
        def _():
            got_l2(c, t)
            total[at] += left2[c, span, :]

        @pl.when(me == 2)
        def _():
            arrived = left2[c, span, :]
            total[at] += pick(arrived, jnp.zeros_like(arrived))

        out_copy(c, t).start()

    def finish_some(k, t):
        f = k - chunks - 3

        @pl.when(f >= 0)
        def _():
            finish(2 * f, t)

            @pl.when(2 * f + 1 < chunks - 1)
            def _():
                finish(2 * f + 1, t)

    def exchange(k, u):
        i, j = k - 1, k - 2

        @pl.when(jnp.logical_and(k >= 1, k <= chunks))
        def _():
            span = pair_of(u)
            added = dot3((far_hi[i, span, :], far_lo[i, span, :]), (own_hi[span, :], own_lo[span, :]), ((0,), (0,)))

            @pl.when(u == 0)
            def _():
                ints[i] = added

            @pl.when(u > 0)
            def _():
                ints[i] += added

            @pl.when(u == PARTS // 2 - 1)
            def _():
                a_copy(i).start()

        @pl.when(jnp.logical_and(k >= 2, k <= chunks + 1))
        def _():
            @pl.when(u == 0)
            def _():
                a_copy(j).wait_recv()
                half[j] = ints[j, pl.ds(mine, share), :] + core_in[j]
                b_copy(j).start()

            @pl.when(u == PARTS // 2 - 1)
            def _():
                b_copy(j).wait_recv()
                at = pl.ds(mine, share)
                single = jnp.full((share, width), odd, jnp.int32).astype(jnp.float32)
                weight = jnp.where(jnp.full((share, width), me % 3, jnp.int32) > 0, 2.0 - single, single)
                for r in range(chunks):
                    cols = slice(r * width, (r + 1) * width)
                    summed = half[j, :, cols] + x_in[j, :, cols]
                    amp[j, at, cols] = weight * (summed / (gap_cols[j, at, :] + own_row[:, cols]))
                c_copy(j).start()

    def on_terms(k, step):
        @pl.when(jnp.logical_and(k >= 3, k <= chunks + 2))
        def _():
            step(k - 3)

    def term_own(u):
        def step(m):
            @pl.when(u == 0)
            def _():
                c_copy(m).wait_recv()
                amp_hi[...], amp_lo[...] = split(amp[m])

            span = pair_of(u)
            total[span, :] += dot3((far_hi[m, span, :], far_lo[m, span, :]), (amp_hi[...], amp_lo[...]), ((1,), (0,)))

        return step

    def term_far(u):
        def step(m):
            span = pair_of(u)
            res[m, span, :] = dot3((own_hi[span, :], own_lo[span, :]), (amp_hi[...], amp_lo[...]), ((1,), (1,)))

        return step

    def prepare(k, t):
        @pl.when(k == 0)
        def _():
            span = band_of(t)
            own_hi[span, :], own_lo[span, :] = split(own[span, :])
            total[span, :] = jnp.zeros((band, tile_width), jnp.float32)

    def send_results(k):
        d = k - chunks

        @pl.when(d >= 0)
        def _():
            @pl.loop(0, PARTS)
            def _(t):
                @pl.when(me < 2)
                def _():
                    l2(piece(res, d, t), d, t).start()

                @pl.when(last)
                def _():
                    r2(piece(res, d, t), d, t).start()

    @pl.loop(0, PARTS)
    def _(t):
        own_copy(t).wait()

    @pl.loop(0, 2 * chunks)
    def _(k):
        send_results(k)

        @pl.loop(0, PARTS // 2)
        def _(u):
            t = 2 * u
            serve(k, t)
            prepare(k, t)
            arrive(k, t)
            on_terms(k, term_own(u))
            finish_some(k, t)
            serve(k, t + 1)
            prepare(k, t + 1)
            arrive(k, t + 1)
            exchange(k, u)
            on_terms(k, term_far(u))
            finish_some(k, t + 1)

        @pl.when(k == 0)
        def _():
            gap_table()

    @pl.when(me == 2)
    def _():
        @pl.loop(0, LAG)
        def _(n):
            serve_left(2 * chunks * PARTS - LAG + n)

    @pl.loop(0, PARTS)
    def _(t):
        finish(chunks - 1, t)

    pltpu.make_async_copy(total, total_out, out_s).wait()

    @pl.when(me < LINE - 1)
    def _():
        remote(left1, left1, l1_s, l1_r.at[0, 0], right).wait_send()
        remote(left2, left2, l2_s, l2_r.at[0, 0], right).wait_send()

    @pl.when(me > 0)
    def _():
        remote(right1, right1, r1_s, r1_r.at[0, 0], left).wait_send()
        remote(right2, right2, r2_s, r2_r.at[0, 0], left).wait_send()

    remote(core_in, core_in, a_s, a_r.at[0], core).wait_send()
    remote(half, x_in, b_s, b_r.at[0], xpeer).wait_send()
    remote(core_in, core_in, c_s, c_r.at[0], core).wait_send()


def local_line(factors, eps_occ, eps_vir, tile_index, pair_offset):
    aux_count = lax.axis_size("aux")
    rows, tile_width = factors.shape
    chunks = tile_width // WIDTH
    f32, half = jnp.float32, jnp.bfloat16
    block = pltpu.VMEM((chunks, rows, WIDTH), f32)
    share = pltpu.VMEM((chunks, WIDTH // 2, tile_width), f32)
    dma = pltpu.SemaphoreType.DMA
    anywhere = pl.BlockSpec(memory_space=pl.ANY)
    pieces = [dma, dma((chunks, PARTS))]
    items = [dma, dma((chunks,))]
    return pl.pallas_call(
        functools.partial(line_kernel, aux_count),
        out_shape=jax.ShapeDtypeStruct((rows, tile_width), f32),
        in_specs=[anywhere] * 5,
        out_specs=anywhere,
        scratch_shapes=[pltpu.VMEM((rows, tile_width), f32)]
        + [block] * 7
        + [pltpu.VMEM((rows, tile_width), f32)]
        + [pltpu.VMEM((rows, tile_width), half)] * 2
        + [pltpu.VMEM((chunks, rows, WIDTH), half)] * 2
        + [pltpu.VMEM((chunks, WIDTH, tile_width), f32), share, share, share]
        + [pltpu.VMEM((chunks, WIDTH, tile_width), f32)]
        + [pltpu.VMEM((WIDTH, tile_width), half)] * 2
        + [pltpu.VMEM((16, WIDTH), f32), pltpu.VMEM((1, tile_width), f32), pltpu.VMEM((chunks, WIDTH, WIDTH), f32)]
        + [pltpu.SMEM(eps_occ.shape, f32), pltpu.SMEM(eps_vir.shape, f32)]
        + [pltpu.SMEM((1,), jnp.int32)] * 2
        + pieces * 4
        + items * 3
        + [dma((PARTS,)), dma((4,)), dma],
        compiler_params=pltpu.CompilerParams(
            collective_id=0, has_side_effects=True, vmem_limit_bytes=56 * 1024 * 1024
        ),
        name="pair_line",
    )(factors, eps_occ, eps_vir, tile_index, pair_offset)


def solution(mesh):
    in_specs = (P(("grp", "aux"), "occ"), P("grp"), P("grp"), P("grp"), P("grp"))
    out_specs = P(("grp", "aux"), "occ")
    body = local_line if mesh.shape["occ"] == LINE and mesh.shape["aux"] == SHARDS else local_ring
    return jax.shard_map(body, mesh=mesh, in_specs=in_specs, out_specs=out_specs, check_vma=False)
```

```python
import functools

import jax
import jax.numpy as jnp
from jax import lax
from jax.experimental import pallas as pl
from jax.experimental.pallas import tpu as pltpu
from jax.sharding import PartitionSpec as P

VT = 192
BLK = 4
DMAX = 3
WIDTH = 128
PARTS = 8
LAG = 2
LINE = 4
SHARDS = 4
MESH = pl.DeviceIdType.MESH

PRECISE = lax.Precision.HIGH


def inner_dot(left, right):
    return lax.dot_general(
        left, right, (((0,), (0,)), ((), ())), precision=PRECISE, preferred_element_type=jnp.float32
    )


def outer_dot(left, right):
    return lax.dot_general(
        left, right, (((1,), (1,)), ((), ())), precision=PRECISE, preferred_element_type=jnp.float32
    )


def gaps_of(vir_energy, energies):
    return (vir_energy[None, :] - energies[:, None]).reshape(-1)


def amplitude_of(own, far, own_gaps, far_gaps, weight):
    aux_count = lax.axis_size("aux")
    aux_rank = lax.axis_index("aux")
    share = far.shape[1] // aux_count
    ints = lax.psum_scatter(inner_dot(far, own), "aux", scatter_dimension=0, tiled=True)
    gaps = lax.dynamic_slice_in_dim(far_gaps, aux_rank * share, share)
    amplitude = jnp.where(weight > 0, weight * (ints / (gaps[:, None] + own_gaps[None, :])), 0.0)
    return lax.all_gather(amplitude, "aux", axis=0, tiled=True)


def term(far, amplitude):
    return jnp.dot(far, amplitude, precision=PRECISE, preferred_element_type=jnp.float32)


def local_ring(factors, eps_occ, eps_vir, tile_index, pair_offset):
    count = lax.axis_size("occ")
    me = lax.axis_index("occ")
    vir_energy = lax.dynamic_slice_in_dim(eps_vir, tile_index[0] * VT, VT)
    energy = eps_occ.reshape(count, BLK)
    own_gaps = gaps_of(vir_energy, energy[me])
    offset = pair_offset[0]
    total = jnp.zeros_like(factors)
    for sign in (1, -1):
        far = factors
        held = factors
        for hop in range(1, DMAX + 1):
            held = lax.ppermute(held, "occ", [(i, (i + sign) % count) for i in range(count)])
            far = jnp.where(offset == hop, held, far)
        far_gaps = gaps_of(vir_energy, energy[(me - sign * offset) % count])
        total = total + term(far, amplitude_of(factors, far, own_gaps, far_gaps, jnp.float32(1)))
    return total


def split(x):
    high = x.astype(jnp.bfloat16)
    return high, (x - high.astype(jnp.float32)).astype(jnp.bfloat16)


def dot3(left, right, dims):
    dot = functools.partial(lax.dot_general, dimension_numbers=(dims, ((), ())), preferred_element_type=jnp.float32)
    return dot(left[0], right[0]) + (dot(left[0], right[1]) + dot(left[1], right[0]))


def line_kernel(
    aux, own_hbm, occ_hbm, vir_hbm, tile_hbm, offset_hbm, total,
    own, right1, left1, right2, left2, res, relay1, relay2, own_hi, own_lo, far_hi, far_lo,
    ints, core_in, half, x_in, amp, amp_hi, amp_lo, table, own_row, gap_cols,
    occ_energy, vir_energy, tile, offset,
    r1_s, r1_r, l1_s, l1_r, r2_s, r2_r, l2_s, l2_r,
    a_s, a_r, b_s, b_r, c_s, c_r, own_s, small_s,
):
    chunks, rows, width = right1.shape
    tile_width = own.shape[1]
    share = width // 2
    band = rows // PARTS
    pair = 2 * band
    me = lax.axis_index("occ")
    rank = lax.axis_index("aux")
    first, last = me == 0, me == LINE - 1
    left, right = {"occ": me - 1}, {"occ": me + 1}
    to_hub, from_hub = {"occ": me + jnp.where(first, 2, 1)}, {"occ": me - jnp.where(me == 2, 2, 1)}
    core = {"aux": rank + 1 - 2 * (rank % 2)}
    xpeer = {"aux": (rank + 2) % aux}
    mine = pl.multiple_of((rank % 2) * share, share)
    theirs = pl.multiple_of((1 - rank % 2) * share, share)

    def remote(src, dst, send, recv, target):
        return pltpu.make_async_remote_copy(
            src_ref=src, dst_ref=dst, send_sem=send, recv_sem=recv, device_id=target, device_id_type=MESH
        )

    def columns(c):
        return pl.ds(pl.multiple_of(c * width, width), width)

    def band_of(t):
        return pl.ds(pl.multiple_of(t * band, band), band)

    def pair_of(u):
        return pl.ds(pl.multiple_of(u * pair, pair), pair)

    def piece(ref, c, t):
        return ref.at[c, band_of(t)]

    def own_piece(c, t):
        return own_hbm.at[band_of(t), columns(c)]

    def r1(src, c, t):
        return remote(src, piece(right1, c, t), r1_s, r1_r.at[c, t], left)

    def l1(src, c, t):
        return remote(src, piece(left1, c, t), l1_s, l1_r.at[c, t], to_hub)

    def r2(src, c, t):
        return remote(src, piece(right2, c, t), r2_s, r2_r.at[c, t], from_hub)

    def l2(src, c, t):
        return remote(src, piece(left2, c, t), l2_s, l2_r.at[c, t], right)

    def got_r1(c, t):
        r1(piece(right1, c, t), c, t).wait_recv()

    def got_l1(c, t):
        l1(piece(left1, c, t), c, t).wait_recv()

    def got_r2(c, t):
        r2(piece(right2, c, t), c, t).wait_recv()

    def got_l2(c, t):
        l2(piece(left2, c, t), c, t).wait_recv()

    def a_copy(i):
        return remote(ints.at[i, pl.ds(theirs, share)], core_in.at[i], a_s, a_r.at[i], core)

    def b_copy(i):
        return remote(half.at[i], x_in.at[i], b_s, b_r.at[i], xpeer)

    def c_copy(i):
        rows_of = amp.at[i, pl.ds(mine, share)]
        return remote(rows_of, rows_of, c_s, c_r.at[i], core)

    def own_copy(t):
        return pltpu.make_async_copy(own_hbm.at[band_of(t)], own.at[band_of(t)], own_s.at[t])

    def small_copies():
        pairs = ((occ_hbm, occ_energy), (vir_hbm, vir_energy), (tile_hbm, tile), (offset_hbm, offset))
        return [pltpu.make_async_copy(src, dst, small_s.at[n]) for n, (src, dst) in enumerate(pairs)]

    for copy in small_copies():
        copy.start()

    @pl.loop(0, PARTS)
    def _(t):
        own_copy(t).start()

    barrier = pltpu.get_barrier_semaphore()
    for target in (core, xpeer):
        pl.semaphore_signal(barrier, inc=1, device_id=target, device_id_type=MESH)

    for block, greeted in enumerate(((1, 2), (0, 2), (0, 1, 3), (2,))):

        @pl.when(me == block)
        def _():
            for other in greeted:
                pl.semaphore_signal(barrier, inc=1, device_id={"occ": other}, device_id_type=MESH)
            pl.semaphore_wait(barrier, 2 + len(greeted))

    def send_own(c, t):
        @pl.when(first)
        def _():
            l1(own_piece(c, t), c, t).start()

        @pl.when(jnp.logical_or(me == 1, last))
        def _():
            r1(own_piece(c, t), c, t).start()

    @pl.loop(0, PARTS)
    def _(t):
        send_own(0, t)

    for copy in small_copies():
        copy.wait()

    odd = offset[0] & 1

    def pick(odd_one, even_one):
        return jnp.where(jnp.full(odd_one.shape, odd, jnp.int32) > 0, odd_one, even_one)

    def gap_table():
        tall = (8, width)
        place = lax.broadcasted_iota(jnp.int32, tall, 0) * width + lax.broadcasted_iota(jnp.int32, tall, 1)
        orbital = jnp.zeros(tall, jnp.int32)
        for n in range(1, BLK):
            orbital = orbital + jnp.where(place >= n * VT, 1, 0)
        virtual = place - orbital * VT
        base = tile[0] * VT
        energies = lax.fori_loop(
            0, VT, lambda a, so_far: jnp.where(virtual == a, vir_energy[base + a], so_far), jnp.zeros(tall, jnp.float32)
        )

        def of_block(block):
            value = jnp.zeros(tall, jnp.float32)
            for n in range(BLK):
                value = jnp.where(orbital == n, occ_energy[block * BLK + n], value)
            return value

        odd_block = (me + 1) % LINE
        even_block = jnp.where(first, 1, jnp.where(me == 1, LINE - 1, 0))
        table[0:8, :] = energies - of_block(me)
        table[8:16, :] = energies - pick(of_block(odd_block), of_block(even_block))
        for r in range(chunks):
            own_row[:, r * width : (r + 1) * width] = table[r : r + 1, :]

        @pl.loop(0, chunks)
        def _(i):
            gap_cols[i] = jnp.broadcast_to(table[pl.ds(8 + i, 1), :], (width, width)).T

    def split_far(c, t, far):
        span = band_of(t)
        far_hi[c, span, :], far_lo[c, span, :] = split(far)

    def serve_left(s):
        c, t = s // PARTS, s % PARTS

        @pl.when(jnp.logical_and(s >= 0, c < chunks))
        def _():
            got_l1(c, t)
            l1(piece(left1, c, t), c, t).start()
            span = band_of(t)
            split_far(c, t, pick(right1[c, span, :], left1[c, span, :]))

        @pl.when(c >= chunks)
        def _():
            d = c - chunks
            span = band_of(t)
            got_l2(d, t)
            relay2[d, span, :] = pick(res[d, span, :], left2[d, span, :])
            l2(piece(relay2, d, t), d, t).start()

    def serve(k, t):
        span = band_of(t)

        @pl.when(me == 2)
        def _():
            @pl.when(k < chunks)
            def _():
                got_r1(k, t)
                relay1[k, span, :] = pick(own[span, columns(k)], right1[k, span, :])
                r1(piece(relay1, k, t), k, t).start()

            @pl.when(k >= chunks)
            def _():
                d = k - chunks
                got_r2(d, t)
                right2[d, span, :] = pick(right2[d, span, :], res[d, span, :])
                r2(piece(right2, d, t), d, t).start()

            serve_left(k * PARTS + t - LAG)

    def arrive(k, t):
        c = k - 1
        span = band_of(t)

        @pl.when(jnp.logical_and(k >= 1, k <= chunks))
        def _():
            @pl.when(me < 2)
            def _():
                got_r1(c, t)
                split_far(c, t, right1[c, span, :])

            @pl.when(last)
            def _():
                got_l1(c, t)
                split_far(c, t, left1[c, span, :])

        @pl.when(k + 1 < chunks)
        def _():
            send_own(k + 1, t)

    def finish(c, t):
        span = band_of(t)
        at = (span, columns(c))

        @pl.when(first)
        def _():
            got_r2(c, t)
            total[at] += right2[c, span, :]

        @pl.when(jnp.logical_or(me == 1, last))
        def _():
            got_l2(c, t)
            total[at] += left2[c, span, :]

        @pl.when(me == 2)
        def _():
            arrived = left2[c, span, :]
            total[at] += pick(arrived, jnp.zeros_like(arrived))


    def finish_some(k, t):
        f = k - chunks - 3

        @pl.when(f >= 0)
        def _():
            finish(2 * f, t)

            @pl.when(2 * f + 1 < chunks - 1)
            def _():
                finish(2 * f + 1, t)

    def exchange(k, u):
        i, j = k - 1, k - 2

        @pl.when(jnp.logical_and(k >= 1, k <= chunks))
        def _():
            span = pair_of(u)
            added = dot3((far_hi[i, span, :], far_lo[i, span, :]), (own_hi[span, :], own_lo[span, :]), ((0,), (0,)))

            @pl.when(u == 0)
            def _():
                ints[i] = added

            @pl.when(u > 0)
            def _():
                ints[i] += added

            @pl.when(u == PARTS // 2 - 1)
            def _():
                a_copy(i).start()

        @pl.when(jnp.logical_and(k >= 2, k <= chunks + 1))
        def _():
            @pl.when(u == 0)
            def _():
                a_copy(j).wait_recv()
                half[j] = ints[j, pl.ds(mine, share), :] + core_in[j]
                b_copy(j).start()

            @pl.when(u == PARTS // 2 - 1)
            def _():
                b_copy(j).wait_recv()
                at = pl.ds(mine, share)
                single = jnp.full((share, width), odd, jnp.int32).astype(jnp.float32)
                weight = jnp.where(jnp.full((share, width), me % 3, jnp.int32) > 0, 2.0 - single, single)
                for r in range(chunks):
                    cols = slice(r * width, (r + 1) * width)
                    summed = half[j, :, cols] + x_in[j, :, cols]
                    amp[j, at, cols] = weight * (summed / (gap_cols[j, at, :] + own_row[:, cols]))
                c_copy(j).start()

    def on_terms(k, step):
        @pl.when(jnp.logical_and(k >= 3, k <= chunks + 2))
        def _():
            step(k - 3)

    def term_own(u):
        def step(m):
            @pl.when(u == 0)
            def _():
                c_copy(m).wait_recv()
                amp_hi[...], amp_lo[...] = split(amp[m])

            span = pair_of(u)
            total[span, :] += dot3((far_hi[m, span, :], far_lo[m, span, :]), (amp_hi[...], amp_lo[...]), ((1,), (0,)))

        return step

    def term_far(u):
        def step(m):
            span = pair_of(u)
            res[m, span, :] = dot3((own_hi[span, :], own_lo[span, :]), (amp_hi[...], amp_lo[...]), ((1,), (1,)))

        return step

    def prepare(k, t):
        @pl.when(k == 0)
        def _():
            span = band_of(t)
            own_hi[span, :], own_lo[span, :] = split(own[span, :])
            total[span, :] = jnp.zeros((band, tile_width), jnp.float32)

    def send_results(k):
        d = k - chunks

        @pl.when(d >= 0)
        def _():
            @pl.loop(0, PARTS)
            def _(t):
                @pl.when(me < 2)
                def _():
                    l2(piece(res, d, t), d, t).start()

                @pl.when(last)
                def _():
                    r2(piece(res, d, t), d, t).start()

    @pl.loop(0, PARTS)
    def _(t):
        own_copy(t).wait()

    @pl.loop(0, 2 * chunks)
    def _(k):
        send_results(k)

        @pl.loop(0, PARTS // 2)
        def _(u):
            t = 2 * u
            serve(k, t)
            prepare(k, t)
            arrive(k, t)
            on_terms(k, term_own(u))
            finish_some(k, t)
            serve(k, t + 1)
            prepare(k, t + 1)
            arrive(k, t + 1)
            exchange(k, u)
            on_terms(k, term_far(u))
            finish_some(k, t + 1)

        @pl.when(k == 0)
        def _():
            gap_table()

    @pl.when(me == 2)
    def _():
        @pl.loop(0, LAG)
        def _(n):
            serve_left(2 * chunks * PARTS - LAG + n)

    @pl.loop(0, PARTS)
    def _(t):
        finish(chunks - 1, t)

    @pl.when(me < LINE - 1)
    def _():
        remote(left2, left2, l2_s, l2_r.at[0, 0], right).wait_send()

    @pl.when(me > 0)
    def _():
        remote(right1, right1, r1_s, r1_r.at[0, 0], left).wait_send()

    @pl.when(me % 2 == 0)
    def _():
        remote(left1, left1, l1_s, l1_r.at[0, 0], to_hub).wait_send()

    @pl.when(me >= 2)
    def _():
        remote(right2, right2, r2_s, r2_r.at[0, 0], from_hub).wait_send()

    remote(core_in, core_in, a_s, a_r.at[0], core).wait_send()
    remote(half, x_in, b_s, b_r.at[0], xpeer).wait_send()
    remote(core_in, core_in, c_s, c_r.at[0], core).wait_send()


def local_line(factors, eps_occ, eps_vir, tile_index, pair_offset):
    aux_count = lax.axis_size("aux")
    rows, tile_width = factors.shape
    chunks = tile_width // WIDTH
    f32, half = jnp.float32, jnp.bfloat16
    block = pltpu.VMEM((chunks, rows, WIDTH), f32)
    share = pltpu.VMEM((chunks, WIDTH // 2, tile_width), f32)
    dma = pltpu.SemaphoreType.DMA
    anywhere = pl.BlockSpec(memory_space=pl.ANY)
    pieces = [dma, dma((chunks, PARTS))]
    items = [dma, dma((chunks,))]
    pinned = [pltpu.with_memory_space_constraint(x, pltpu.HBM) for x in (factors, eps_occ, eps_vir)]
    return pl.pallas_call(
        functools.partial(line_kernel, aux_count),
        out_shape=pltpu.VMEM((rows, tile_width), f32),
        in_specs=[anywhere] * 5,
        out_specs=pl.BlockSpec(memory_space=pltpu.VMEM),
        scratch_shapes=[pltpu.VMEM((rows, tile_width), f32)]
        + [block] * 7
        + [pltpu.VMEM((rows, tile_width), half)] * 2
        + [pltpu.VMEM((chunks, rows, WIDTH), half)] * 2
        + [pltpu.VMEM((chunks, WIDTH, tile_width), f32), share, share, share]
        + [pltpu.VMEM((chunks, WIDTH, tile_width), f32)]
        + [pltpu.VMEM((WIDTH, tile_width), half)] * 2
        + [pltpu.VMEM((16, WIDTH), f32), pltpu.VMEM((1, tile_width), f32), pltpu.VMEM((chunks, WIDTH, WIDTH), f32)]
        + [pltpu.SMEM(eps_occ.shape, f32), pltpu.SMEM(eps_vir.shape, f32)]
        + [pltpu.SMEM((1,), jnp.int32)] * 2
        + pieces * 4
        + items * 3
        + [dma((PARTS,)), dma((4,))],
        compiler_params=pltpu.CompilerParams(
            collective_id=0, has_side_effects=True, vmem_limit_bytes=50 * 1024 * 1024
        ),
        name="pair_line",
    )(*pinned, tile_index, pair_offset)


def solution(mesh):
    in_specs = (P(("grp", "aux"), "occ"), P("grp"), P("grp"), P("grp"), P("grp"))
    out_specs = P(("grp", "aux"), "occ")
    body = local_line if mesh.shape["occ"] == LINE and mesh.shape["aux"] == SHARDS else local_ring
    return jax.shard_map(body, mesh=mesh, in_specs=in_specs, out_specs=out_specs, check_vma=False)
```

```python
import functools

import jax
import jax.numpy as jnp
from jax import lax
from jax.experimental import pallas as pl
from jax.experimental.pallas import tpu as pltpu
from jax.sharding import PartitionSpec as P

VT = 192
BLK = 4
DMAX = 3
WIDTH = 128
PARTS = 8
LAG = 1
LINE = 4
SHARDS = 4
MESH = pl.DeviceIdType.MESH

PRECISE = lax.Precision.HIGH


def inner_dot(left, right):
    return lax.dot_general(
        left, right, (((0,), (0,)), ((), ())), precision=PRECISE, preferred_element_type=jnp.float32
    )


def outer_dot(left, right):
    return lax.dot_general(
        left, right, (((1,), (1,)), ((), ())), precision=PRECISE, preferred_element_type=jnp.float32
    )


def gaps_of(vir_energy, energies):
    return (vir_energy[None, :] - energies[:, None]).reshape(-1)


def amplitude_of(own, far, own_gaps, far_gaps, weight):
    aux_count = lax.axis_size("aux")
    aux_rank = lax.axis_index("aux")
    share = far.shape[1] // aux_count
    ints = lax.psum_scatter(inner_dot(far, own), "aux", scatter_dimension=0, tiled=True)
    gaps = lax.dynamic_slice_in_dim(far_gaps, aux_rank * share, share)
    amplitude = jnp.where(weight > 0, weight * (ints / (gaps[:, None] + own_gaps[None, :])), 0.0)
    return lax.all_gather(amplitude, "aux", axis=0, tiled=True)


def term(far, amplitude):
    return jnp.dot(far, amplitude, precision=PRECISE, preferred_element_type=jnp.float32)


def local_ring(factors, eps_occ, eps_vir, tile_index, pair_offset):
    count = lax.axis_size("occ")
    me = lax.axis_index("occ")
    vir_energy = lax.dynamic_slice_in_dim(eps_vir, tile_index[0] * VT, VT)
    energy = eps_occ.reshape(count, BLK)
    own_gaps = gaps_of(vir_energy, energy[me])
    offset = pair_offset[0]
    total = jnp.zeros_like(factors)
    for sign in (1, -1):
        far = factors
        held = factors
        for hop in range(1, DMAX + 1):
            held = lax.ppermute(held, "occ", [(i, (i + sign) % count) for i in range(count)])
            far = jnp.where(offset == hop, held, far)
        far_gaps = gaps_of(vir_energy, energy[(me - sign * offset) % count])
        total = total + term(far, amplitude_of(factors, far, own_gaps, far_gaps, jnp.float32(1)))
    return total


def split(x):
    high = x.astype(jnp.bfloat16)
    return high, (x - high.astype(jnp.float32)).astype(jnp.bfloat16)


def dot3(left, right, dims):
    dot = functools.partial(lax.dot_general, dimension_numbers=(dims, ((), ())), preferred_element_type=jnp.float32)
    return dot(left[0], right[0]) + (dot(left[0], right[1]) + dot(left[1], right[0]))


def line_kernel(
    aux, own_hbm, occ_hbm, vir_hbm, tile_hbm, offset_hbm, total,
    own, right1, left1, right2, left2, res, relay1, relay2, own_hi, own_lo, far_hi, far_lo,
    ints, core_in, half, x_in, amp, amp_hi, amp_lo, table, own_row, gap_cols,
    occ_energy, vir_energy, tile, offset,
    r1_s, r1_r, l1_s, l1_r, r2_s, r2_r, l2_s, l2_r,
    a_s, a_r, b_s, b_r, c_s, c_r, own_s, small_s,
):
    chunks, rows, width = right1.shape
    tile_width = own.shape[1]
    share = width // 2
    band = rows // PARTS
    pair = 2 * band
    me = lax.axis_index("occ")
    rank = lax.axis_index("aux")
    first, last = me == 0, me == LINE - 1
    left, right = {"occ": me - 1}, {"occ": me + 1}
    to_hub, from_hub = {"occ": me + jnp.where(first, 2, 1)}, {"occ": me - jnp.where(me == 2, 2, 1)}
    core = {"aux": rank + 1 - 2 * (rank % 2)}
    xpeer = {"aux": (rank + 2) % aux}
    mine = pl.multiple_of((rank % 2) * share, share)
    theirs = pl.multiple_of((1 - rank % 2) * share, share)

    def remote(src, dst, send, recv, target):
        return pltpu.make_async_remote_copy(
            src_ref=src, dst_ref=dst, send_sem=send, recv_sem=recv, device_id=target, device_id_type=MESH
        )

    def columns(c):
        return pl.ds(pl.multiple_of(c * width, width), width)

    def band_of(t):
        return pl.ds(pl.multiple_of(t * band, band), band)

    def pair_of(u):
        return pl.ds(pl.multiple_of(u * pair, pair), pair)

    def piece(ref, c, t):
        return ref.at[c, band_of(t)]

    def own_piece(c, t):
        return own.at[band_of(t), columns(c)]

    def r1(src, c, t):
        return remote(src, piece(right1, c, t), r1_s, r1_r.at[c, t], left)

    def l1(src, c, t):
        return remote(src, piece(left1, c, t), l1_s, l1_r.at[c, t], to_hub)

    def r2(src, c, t):
        return remote(src, piece(right2, c, t), r2_s, r2_r.at[c, t], from_hub)

    def l2(src, c, t):
        return remote(src, piece(left2, c, t), l2_s, l2_r.at[c, t], right)

    def got_r1(c, t):
        r1(piece(right1, c, t), c, t).wait_recv()

    def got_l1(c, t):
        l1(piece(left1, c, t), c, t).wait_recv()

    def got_r2(c, t):
        r2(piece(right2, c, t), c, t).wait_recv()

    def got_l2(c, t):
        l2(piece(left2, c, t), c, t).wait_recv()

    def a_copy(i):
        return remote(ints.at[i, pl.ds(theirs, share)], core_in.at[i], a_s, a_r.at[i], core)

    def b_copy(i):
        return remote(half.at[i], x_in.at[i], b_s, b_r.at[i], xpeer)

    def c_copy(i):
        rows_of = amp.at[i, pl.ds(mine, share)]
        return remote(rows_of, rows_of, c_s, c_r.at[i], core)

    def own_copy(t):
        return pltpu.make_async_copy(own_hbm.at[band_of(t)], own.at[band_of(t)], own_s.at[t])

    def small_copies():
        pairs = ((occ_hbm, occ_energy), (vir_hbm, vir_energy), (tile_hbm, tile), (offset_hbm, offset))
        return [pltpu.make_async_copy(src, dst, small_s.at[n]) for n, (src, dst) in enumerate(pairs)]

    @pl.loop(0, PARTS)
    def _(t):
        own_copy(t).start()

    barrier = pltpu.get_barrier_semaphore()
    for target in (core, xpeer):
        pl.semaphore_signal(barrier, inc=1, device_id=target, device_id_type=MESH)

    for copy in small_copies():
        copy.start()

    for block, greeted in enumerate(((1, 2), (0, 2), (0, 1, 3), (2,))):

        @pl.when(me == block)
        def _():
            for other in greeted:
                pl.semaphore_signal(barrier, inc=1, device_id={"occ": other}, device_id_type=MESH)
            pl.semaphore_wait(barrier, 2 + len(greeted))

    def send_own(c, t):
        @pl.when(first)
        def _():
            l1(own_piece(c, t), c, t).start()

        @pl.when(jnp.logical_or(me == 1, last))
        def _():
            r1(own_piece(c, t), c, t).start()

    @pl.loop(0, PARTS)
    def _(t):
        own_copy(t).wait()
        send_own(0, t)

    for copy in small_copies():
        copy.wait()

    odd = offset[0] & 1

    def pick(odd_one, even_one):
        return jnp.where(jnp.full(odd_one.shape, odd, jnp.int32) > 0, odd_one, even_one)

    def gap_table():
        tall = (8, width)
        place = lax.broadcasted_iota(jnp.int32, tall, 0) * width + lax.broadcasted_iota(jnp.int32, tall, 1)
        orbital = jnp.zeros(tall, jnp.int32)
        for n in range(1, BLK):
            orbital = orbital + jnp.where(place >= n * VT, 1, 0)
        virtual = place - orbital * VT
        base = tile[0] * VT
        energies = lax.fori_loop(
            0, VT, lambda a, so_far: jnp.where(virtual == a, vir_energy[base + a], so_far), jnp.zeros(tall, jnp.float32)
        )

        def of_block(block):
            value = jnp.zeros(tall, jnp.float32)
            for n in range(BLK):
                value = jnp.where(orbital == n, occ_energy[block * BLK + n], value)
            return value

        odd_block = (me + 1) % LINE
        even_block = jnp.where(first, 1, jnp.where(me == 1, LINE - 1, 0))
        table[0:8, :] = energies - of_block(me)
        table[8:16, :] = energies - pick(of_block(odd_block), of_block(even_block))
        for r in range(chunks):
            own_row[:, r * width : (r + 1) * width] = table[r : r + 1, :]

        @pl.loop(0, chunks)
        def _(i):
            gap_cols[i] = jnp.broadcast_to(table[pl.ds(8 + i, 1), :], (width, width)).T

    def split_far(c, t, far):
        span = band_of(t)
        far_hi[c, span, :], far_lo[c, span, :] = split(far)

    def serve_left(s):
        c, t = s // PARTS, s % PARTS

        @pl.when(jnp.logical_and(s >= 0, c < chunks))
        def _():
            got_l1(c, t)
            l1(piece(left1, c, t), c, t).start()
            span = band_of(t)
            split_far(c, t, pick(right1[c, span, :], left1[c, span, :]))

        @pl.when(c >= chunks)
        def _():
            d = c - chunks
            span = band_of(t)
            got_l2(d, t)
            relay2[d, span, :] = pick(res[d, span, :], left2[d, span, :])
            l2(piece(relay2, d, t), d, t).start()

    def serve(k, t):
        span = band_of(t)

        @pl.when(me == 2)
        def _():
            @pl.when(k < chunks)
            def _():
                got_r1(k, t)
                relay1[k, span, :] = pick(own[span, columns(k)], right1[k, span, :])
                r1(piece(relay1, k, t), k, t).start()

            @pl.when(k >= chunks)
            def _():
                d = k - chunks
                got_r2(d, t)
                right2[d, span, :] = pick(right2[d, span, :], res[d, span, :])
                r2(piece(right2, d, t), d, t).start()

            serve_left(k * PARTS + t - LAG)

    def arrive(k, t):
        c = k - 1
        span = band_of(t)

        @pl.when(jnp.logical_and(k >= 1, k <= chunks))
        def _():
            @pl.when(me < 2)
            def _():
                got_r1(c, t)
                split_far(c, t, right1[c, span, :])

            @pl.when(last)
            def _():
                got_l1(c, t)
                split_far(c, t, left1[c, span, :])

        @pl.when(k + 1 < chunks)
        def _():
            send_own(k + 1, t)

    def finish(c, t):
        span = band_of(t)
        at = (span, columns(c))

        @pl.when(first)
        def _():
            got_r2(c, t)
            total[at] += right2[c, span, :]

        @pl.when(jnp.logical_or(me == 1, last))
        def _():
            got_l2(c, t)
            total[at] += left2[c, span, :]

        @pl.when(me == 2)
        def _():
            arrived = left2[c, span, :]
            total[at] += pick(arrived, jnp.zeros_like(arrived))


    def finish_some(k, t):
        f = k - chunks - 3

        @pl.when(f >= 0)
        def _():
            finish(2 * f, t)

            @pl.when(2 * f + 1 < chunks - 1)
            def _():
                finish(2 * f + 1, t)

    def exchange(k, u):
        i, j = k - 1, k - 2

        @pl.when(jnp.logical_and(k >= 1, k <= chunks))
        def _():
            span = pair_of(u)
            added = dot3((far_hi[i, span, :], far_lo[i, span, :]), (own_hi[span, :], own_lo[span, :]), ((0,), (0,)))

            @pl.when(u == 0)
            def _():
                ints[i] = added

            @pl.when(u > 0)
            def _():
                ints[i] += added

            @pl.when(u == PARTS // 2 - 1)
            def _():
                a_copy(i).start()

        @pl.when(jnp.logical_and(k >= 2, k <= chunks + 1))
        def _():
            @pl.when(u == 0)
            def _():
                a_copy(j).wait_recv()
                half[j] = ints[j, pl.ds(mine, share), :] + core_in[j]
                b_copy(j).start()

            @pl.when(u == PARTS // 2 - 1)
            def _():
                b_copy(j).wait_recv()
                at = pl.ds(mine, share)
                single = jnp.full((share, width), odd, jnp.int32).astype(jnp.float32)
                weight = jnp.where(jnp.full((share, width), me % 3, jnp.int32) > 0, 2.0 - single, single)
                for r in range(chunks):
                    cols = slice(r * width, (r + 1) * width)
                    summed = half[j, :, cols] + x_in[j, :, cols]
                    amp[j, at, cols] = weight * (summed / (gap_cols[j, at, :] + own_row[:, cols]))
                c_copy(j).start()

    def on_terms(k, step):
        @pl.when(jnp.logical_and(k >= 3, k <= chunks + 2))
        def _():
            step(k - 3)

    def term_own(u):
        def step(m):
            @pl.when(u == 0)
            def _():
                c_copy(m).wait_recv()
                amp_hi[...], amp_lo[...] = split(amp[m])

            span = pair_of(u)
            total[span, :] += dot3((far_hi[m, span, :], far_lo[m, span, :]), (amp_hi[...], amp_lo[...]), ((1,), (0,)))

        return step

    def term_far(u):
        def step(m):
            span = pair_of(u)
            res[m, span, :] = dot3((own_hi[span, :], own_lo[span, :]), (amp_hi[...], amp_lo[...]), ((1,), (1,)))

        return step

    def prepare(k, t):
        @pl.when(k == 0)
        def _():
            span = band_of(t)
            own_hi[span, :], own_lo[span, :] = split(own[span, :])
            total[span, :] = jnp.zeros((band, tile_width), jnp.float32)

    def send_results(k):
        d = k - chunks

        @pl.when(d >= 0)
        def _():
            @pl.loop(0, PARTS)
            def _(t):
                @pl.when(me < 2)
                def _():
                    l2(piece(res, d, t), d, t).start()

                @pl.when(last)
                def _():
                    r2(piece(res, d, t), d, t).start()

    @pl.loop(0, 2 * chunks)
    def _(k):
        send_results(k)

        @pl.loop(0, PARTS // 2)
        def _(u):
            t = 2 * u
            serve(k, t)
            prepare(k, t)
            arrive(k, t)
            on_terms(k, term_own(u))
            finish_some(k, t)
            serve(k, t + 1)
            prepare(k, t + 1)
            arrive(k, t + 1)
            exchange(k, u)
            on_terms(k, term_far(u))
            finish_some(k, t + 1)

        @pl.when(k == 0)
        def _():
            gap_table()

    @pl.when(me == 2)
    def _():
        @pl.loop(0, LAG)
        def _(n):
            serve_left(2 * chunks * PARTS - LAG + n)

    @pl.loop(0, PARTS)
    def _(t):
        finish(chunks - 1, t)

    @pl.when(me < LINE - 1)
    def _():
        remote(left2, left2, l2_s, l2_r.at[0, 0], right).wait_send()

    @pl.when(me > 0)
    def _():
        remote(right1, right1, r1_s, r1_r.at[0, 0], left).wait_send()

    @pl.when(me % 2 == 0)
    def _():
        remote(left1, left1, l1_s, l1_r.at[0, 0], to_hub).wait_send()

    @pl.when(me >= 2)
    def _():
        remote(right2, right2, r2_s, r2_r.at[0, 0], from_hub).wait_send()

    remote(core_in, core_in, a_s, a_r.at[0], core).wait_send()
    remote(half, x_in, b_s, b_r.at[0], xpeer).wait_send()
    remote(core_in, core_in, c_s, c_r.at[0], core).wait_send()


def local_line(factors, eps_occ, eps_vir, tile_index, pair_offset):
    aux_count = lax.axis_size("aux")
    rows, tile_width = factors.shape
    chunks = tile_width // WIDTH
    f32, half = jnp.float32, jnp.bfloat16
    block = pltpu.VMEM((chunks, rows, WIDTH), f32)
    share = pltpu.VMEM((chunks, WIDTH // 2, tile_width), f32)
    dma = pltpu.SemaphoreType.DMA
    anywhere = pl.BlockSpec(memory_space=pl.ANY)
    pieces = [dma, dma((chunks, PARTS))]
    items = [dma, dma((chunks,))]
    pinned = [pltpu.with_memory_space_constraint(x, pltpu.HBM) for x in (factors, eps_occ, eps_vir)]
    return pl.pallas_call(
        functools.partial(line_kernel, aux_count),
        out_shape=pltpu.VMEM((rows, tile_width), f32),
        in_specs=[anywhere] * 5,
        out_specs=pl.BlockSpec(memory_space=pltpu.VMEM),
        scratch_shapes=[pltpu.VMEM((rows, tile_width), f32)]
        + [block] * 7
        + [pltpu.VMEM((rows, tile_width), half)] * 2
        + [pltpu.VMEM((chunks, rows, WIDTH), half)] * 2
        + [pltpu.VMEM((chunks, WIDTH, tile_width), f32), share, share, share]
        + [pltpu.VMEM((chunks, WIDTH, tile_width), f32)]
        + [pltpu.VMEM((WIDTH, tile_width), half)] * 2
        + [pltpu.VMEM((16, WIDTH), f32), pltpu.VMEM((1, tile_width), f32), pltpu.VMEM((chunks, WIDTH, WIDTH), f32)]
        + [pltpu.SMEM(eps_occ.shape, f32), pltpu.SMEM(eps_vir.shape, f32)]
        + [pltpu.SMEM((1,), jnp.int32)] * 2
        + pieces * 4
        + items * 3
        + [dma((PARTS,)), dma((4,))],
        compiler_params=pltpu.CompilerParams(
            collective_id=0, has_side_effects=True, vmem_limit_bytes=50 * 1024 * 1024
        ),
        name="pair_line",
    )(*pinned, tile_index, pair_offset)


def solution(mesh):
    in_specs = (P(("grp", "aux"), "occ"), P("grp"), P("grp"), P("grp"), P("grp"))
    out_specs = P(("grp", "aux"), "occ")
    body = local_line if mesh.shape["occ"] == LINE and mesh.shape["aux"] == SHARDS else local_ring
    return jax.shard_map(body, mesh=mesh, in_specs=in_specs, out_specs=out_specs, check_vma=False)
```

```python
import functools

import jax
import jax.numpy as jnp
from jax import lax
from jax.experimental import pallas as pl
from jax.experimental.pallas import tpu as pltpu
from jax.sharding import PartitionSpec as P

VT = 192
BLK = 4
DMAX = 3
WIDTH = 128
PARTS = 8
LAG = 1
LINE = 4
SHARDS = 4
MESH = pl.DeviceIdType.MESH

PRECISE = lax.Precision.HIGH


def inner_dot(left, right):
    return lax.dot_general(
        left, right, (((0,), (0,)), ((), ())), precision=PRECISE, preferred_element_type=jnp.float32
    )


def outer_dot(left, right):
    return lax.dot_general(
        left, right, (((1,), (1,)), ((), ())), precision=PRECISE, preferred_element_type=jnp.float32
    )


def gaps_of(vir_energy, energies):
    return (vir_energy[None, :] - energies[:, None]).reshape(-1)


def amplitude_of(own, far, own_gaps, far_gaps, weight):
    aux_count = lax.axis_size("aux")
    aux_rank = lax.axis_index("aux")
    share = far.shape[1] // aux_count
    ints = lax.psum_scatter(inner_dot(far, own), "aux", scatter_dimension=0, tiled=True)
    gaps = lax.dynamic_slice_in_dim(far_gaps, aux_rank * share, share)
    amplitude = jnp.where(weight > 0, weight * (ints / (gaps[:, None] + own_gaps[None, :])), 0.0)
    return lax.all_gather(amplitude, "aux", axis=0, tiled=True)


def term(far, amplitude):
    return jnp.dot(far, amplitude, precision=PRECISE, preferred_element_type=jnp.float32)


def local_ring(factors, eps_occ, eps_vir, tile_index, pair_offset):
    count = lax.axis_size("occ")
    me = lax.axis_index("occ")
    vir_energy = lax.dynamic_slice_in_dim(eps_vir, tile_index[0] * VT, VT)
    energy = eps_occ.reshape(count, BLK)
    own_gaps = gaps_of(vir_energy, energy[me])
    offset = pair_offset[0]
    total = jnp.zeros_like(factors)
    for sign in (1, -1):
        far = factors
        held = factors
        for hop in range(1, DMAX + 1):
            held = lax.ppermute(held, "occ", [(i, (i + sign) % count) for i in range(count)])
            far = jnp.where(offset == hop, held, far)
        far_gaps = gaps_of(vir_energy, energy[(me - sign * offset) % count])
        total = total + term(far, amplitude_of(factors, far, own_gaps, far_gaps, jnp.float32(1)))
    return total


def split(x):
    high = x.astype(jnp.bfloat16)
    return high, (x - high.astype(jnp.float32)).astype(jnp.bfloat16)


def dot3(left, right, dims):
    dot = functools.partial(lax.dot_general, dimension_numbers=(dims, ((), ())), preferred_element_type=jnp.float32)
    return dot(left[0], right[0]) + (dot(left[0], right[1]) + dot(left[1], right[0]))


def line_kernel(
    aux, own_hbm, occ_hbm, vir_hbm, tile_hbm, offset_hbm, total,
    own, right1, left1, right2, left2, res, relay1, relay2, own_hi, own_lo, far_hi, far_lo,
    ints, core_in, half, x_in, amp, amp_hi, amp_lo, table, own_row, gap_cols,
    occ_energy, vir_energy, tile, offset,
    r1_s, r1_r, l1_s, l1_r, r2_s, r2_r, l2_s, l2_r,
    a_s, a_r, b_s, b_r, c_s, c_r, own_s, small_s,
):
    chunks, rows, width = right1.shape
    tile_width = own.shape[1]
    share = width // 2
    band = rows // PARTS
    pair = 2 * band
    me = lax.axis_index("occ")
    rank = lax.axis_index("aux")
    first, last = me == 0, me == LINE - 1
    left, right = {"occ": (me + LINE - 1) % LINE}, {"occ": (me + 1) % LINE}
    to_hub = {"occ": (me + jnp.where(first, 2, 1)) % LINE}
    from_hub = {"occ": (me + LINE - jnp.where(me == 2, 2, 1)) % LINE}
    core = {"aux": rank + 1 - 2 * (rank % 2)}
    xpeer = {"aux": (rank + 2) % aux}
    mine = pl.multiple_of((rank % 2) * share, share)
    theirs = pl.multiple_of((1 - rank % 2) * share, share)

    def remote(src, dst, send, recv, target):
        return pltpu.make_async_remote_copy(
            src_ref=src, dst_ref=dst, send_sem=send, recv_sem=recv, device_id=target, device_id_type=MESH
        )

    def columns(c):
        return pl.ds(pl.multiple_of(c * width, width), width)

    def band_of(t):
        return pl.ds(pl.multiple_of(t * band, band), band)

    def pair_of(u):
        return pl.ds(pl.multiple_of(u * pair, pair), pair)

    def piece(ref, c, t):
        return ref.at[c, band_of(t)]

    def own_piece(c, t):
        return own.at[band_of(t), columns(c)]

    def r1(src, c, t):
        return remote(src, piece(right1, c, t), r1_s, r1_r.at[c, t], left)

    def l1(src, c, t):
        return remote(src, piece(left1, c, t), l1_s, l1_r.at[c, t], to_hub)

    def r2(src, c, t):
        return remote(src, piece(right2, c, t), r2_s, r2_r.at[c, t], from_hub)

    def l2(src, c, t):
        return remote(src, piece(left2, c, t), l2_s, l2_r.at[c, t], right)

    def got_r1(c, t):
        r1(piece(right1, c, t), c, t).wait_recv()

    def got_l1(c, t):
        l1(piece(left1, c, t), c, t).wait_recv()

    def got_r2(c, t):
        r2(piece(right2, c, t), c, t).wait_recv()

    def got_l2(c, t):
        l2(piece(left2, c, t), c, t).wait_recv()

    def a_copy(i):
        return remote(ints.at[i, pl.ds(theirs, share)], core_in.at[i], a_s, a_r.at[i], core)

    def b_copy(i):
        return remote(half.at[i], x_in.at[i], b_s, b_r.at[i], xpeer)

    def c_copy(i):
        rows_of = amp.at[i, pl.ds(mine, share)]
        return remote(rows_of, rows_of, c_s, c_r.at[i], core)

    def own_copy(t):
        return pltpu.make_async_copy(own_hbm.at[band_of(t)], own.at[band_of(t)], own_s.at[t])

    def small_copies():
        pairs = ((occ_hbm, occ_energy), (vir_hbm, vir_energy), (tile_hbm, tile), (offset_hbm, offset))
        return [pltpu.make_async_copy(src, dst, small_s.at[n]) for n, (src, dst) in enumerate(pairs)]

    @pl.loop(0, PARTS)
    def _(t):
        own_copy(t).start()

    barrier = pltpu.get_barrier_semaphore()
    for target in (core, xpeer):
        pl.semaphore_signal(barrier, inc=1, device_id=target, device_id_type=MESH)

    for copy in small_copies():
        copy.start()

    for block, greeted in enumerate(((1, 2), (0, 2), (0, 1, 3), (2,))):

        @pl.when(me == block)
        def _():
            for other in greeted:
                pl.semaphore_signal(barrier, inc=1, device_id={"occ": other}, device_id_type=MESH)
            pl.semaphore_wait(barrier, 2 + len(greeted))

    def send_own(c, t):
        @pl.when(first)
        def _():
            l1(own_piece(c, t), c, t).start()

        @pl.when(jnp.logical_or(me == 1, last))
        def _():
            r1(own_piece(c, t), c, t).start()

    @pl.loop(0, PARTS)
    def _(t):
        own_copy(t).wait()
        send_own(0, t)

    for copy in small_copies():
        copy.wait()

    odd = offset[0] & 1

    def pick(odd_one, even_one):
        return jnp.where(jnp.full(odd_one.shape, odd, jnp.int32) > 0, odd_one, even_one)

    def gap_table():
        tall = (8, width)
        place = lax.broadcasted_iota(jnp.int32, tall, 0) * width + lax.broadcasted_iota(jnp.int32, tall, 1)
        orbital = jnp.zeros(tall, jnp.int32)
        for n in range(1, BLK):
            orbital = orbital + jnp.where(place >= n * VT, 1, 0)
        virtual = place - orbital * VT
        base = tile[0] * VT
        energies = lax.fori_loop(
            0, VT, lambda a, so_far: jnp.where(virtual == a, vir_energy[base + a], so_far), jnp.zeros(tall, jnp.float32)
        )

        def of_block(block):
            value = jnp.zeros(tall, jnp.float32)
            for n in range(BLK):
                value = jnp.where(orbital == n, occ_energy[block * BLK + n], value)
            return value

        odd_block = (me + 1) % LINE
        even_block = jnp.where(first, 1, jnp.where(me == 1, LINE - 1, 0))
        table[0:8, :] = energies - of_block(me)
        table[8:16, :] = energies - pick(of_block(odd_block), of_block(even_block))
        for r in range(chunks):
            own_row[:, r * width : (r + 1) * width] = table[r : r + 1, :]

        @pl.loop(0, chunks)
        def _(i):
            gap_cols[i] = jnp.broadcast_to(table[pl.ds(8 + i, 1), :], (width, width)).T

    def split_far(c, t, far):
        span = band_of(t)
        far_hi[c, span, :], far_lo[c, span, :] = split(far)

    def serve_left(s):
        c, t = s // PARTS, s % PARTS

        @pl.when(jnp.logical_and(s >= 0, c < chunks))
        def _():
            got_l1(c, t)
            l1(piece(left1, c, t), c, t).start()
            span = band_of(t)
            split_far(c, t, pick(right1[c, span, :], left1[c, span, :]))

        @pl.when(c >= chunks)
        def _():
            d = c - chunks
            span = band_of(t)
            got_l2(d, t)
            relay2[d, span, :] = pick(res[d, span, :], left2[d, span, :])
            l2(piece(relay2, d, t), d, t).start()

    def serve(k, t):
        span = band_of(t)

        @pl.when(me == 2)
        def _():
            @pl.when(k < chunks)
            def _():
                got_r1(k, t)
                relay1[k, span, :] = pick(own[span, columns(k)], right1[k, span, :])
                r1(piece(relay1, k, t), k, t).start()

            @pl.when(k >= chunks)
            def _():
                d = k - chunks
                got_r2(d, t)
                right2[d, span, :] = pick(right2[d, span, :], res[d, span, :])
                r2(piece(right2, d, t), d, t).start()

            serve_left(k * PARTS + t - LAG)

    def arrive(k, t):
        c = k - 1
        span = band_of(t)

        @pl.when(jnp.logical_and(k >= 1, k <= chunks))
        def _():
            @pl.when(me < 2)
            def _():
                got_r1(c, t)
                split_far(c, t, right1[c, span, :])

            @pl.when(last)
            def _():
                got_l1(c, t)
                split_far(c, t, left1[c, span, :])

        @pl.when(k + 1 < chunks)
        def _():
            send_own(k + 1, t)

    def finish(c, t):
        span = band_of(t)
        at = (span, columns(c))

        @pl.when(first)
        def _():
            got_r2(c, t)
            total[at] += right2[c, span, :]

        @pl.when(jnp.logical_or(me == 1, last))
        def _():
            got_l2(c, t)
            total[at] += left2[c, span, :]

        @pl.when(me == 2)
        def _():
            arrived = left2[c, span, :]
            total[at] += pick(arrived, jnp.zeros_like(arrived))


    def finish_some(k, t):
        f = k - chunks - 3

        @pl.when(f >= 0)
        def _():
            finish(2 * f, t)

            @pl.when(2 * f + 1 < chunks - 1)
            def _():
                finish(2 * f + 1, t)

    def exchange(k, u):
        i, j = k - 1, k - 2

        @pl.when(jnp.logical_and(k >= 1, k <= chunks))
        def _():
            span = pair_of(u)
            added = dot3((far_hi[i, span, :], far_lo[i, span, :]), (own_hi[span, :], own_lo[span, :]), ((0,), (0,)))

            @pl.when(u == 0)
            def _():
                ints[i] = added

            @pl.when(u > 0)
            def _():
                ints[i] += added

            @pl.when(u == PARTS // 2 - 1)
            def _():
                a_copy(i).start()

        @pl.when(jnp.logical_and(k >= 2, k <= chunks + 1))
        def _():
            @pl.when(u == 0)
            def _():
                a_copy(j).wait_recv()
                half[j] = ints[j, pl.ds(mine, share), :] + core_in[j]
                b_copy(j).start()

            @pl.when(u == PARTS // 2 - 1)
            def _():
                b_copy(j).wait_recv()
                at = pl.ds(mine, share)
                single = jnp.full((share, width), odd, jnp.int32).astype(jnp.float32)
                weight = jnp.where(jnp.full((share, width), me % 3, jnp.int32) > 0, 2.0 - single, single)
                for r in range(chunks):
                    cols = slice(r * width, (r + 1) * width)
                    summed = half[j, :, cols] + x_in[j, :, cols]
                    amp[j, at, cols] = weight * (summed / (gap_cols[j, at, :] + own_row[:, cols]))
                c_copy(j).start()

    def on_terms(k, step):
        @pl.when(jnp.logical_and(k >= 3, k <= chunks + 2))
        def _():
            step(k - 3)

    def term_own(u):
        def step(m):
            @pl.when(u == 0)
            def _():
                c_copy(m).wait_recv()
                amp_hi[...], amp_lo[...] = split(amp[m])

            span = pair_of(u)
            total[span, :] += dot3((far_hi[m, span, :], far_lo[m, span, :]), (amp_hi[...], amp_lo[...]), ((1,), (0,)))

        return step

    def term_far(u):
        def step(m):
            span = pair_of(u)
            res[m, span, :] = dot3((own_hi[span, :], own_lo[span, :]), (amp_hi[...], amp_lo[...]), ((1,), (1,)))

        return step

    def prepare(k, t):
        @pl.when(k == 0)
        def _():
            span = band_of(t)
            own_hi[span, :], own_lo[span, :] = split(own[span, :])
            total[span, :] = jnp.zeros((band, tile_width), jnp.float32)

    def send_results(k):
        d = k - chunks

        @pl.when(d >= 0)
        def _():
            @pl.loop(0, PARTS)
            def _(t):
                @pl.when(me < 2)
                def _():
                    l2(piece(res, d, t), d, t).start()

                @pl.when(last)
                def _():
                    r2(piece(res, d, t), d, t).start()

    @pl.loop(0, 2 * chunks)
    def _(k):
        send_results(k)

        @pl.loop(0, PARTS // 2)
        def _(u):
            t = 2 * u
            serve(k, t)
            prepare(k, t)
            arrive(k, t)
            on_terms(k, term_own(u))
            finish_some(k, t)
            serve(k, t + 1)
            prepare(k, t + 1)
            arrive(k, t + 1)
            exchange(k, u)
            on_terms(k, term_far(u))
            finish_some(k, t + 1)

        @pl.when(k == 0)
        def _():
            gap_table()

    @pl.when(me == 2)
    def _():
        @pl.loop(0, LAG)
        def _(n):
            serve_left(2 * chunks * PARTS - LAG + n)

    @pl.loop(0, PARTS)
    def _(t):
        finish(chunks - 1, t)

    @pl.when(me < LINE - 1)
    def _():
        remote(left2, left2, l2_s, l2_r.at[0, 0], right).wait_send()

    @pl.when(me > 0)
    def _():
        remote(right1, right1, r1_s, r1_r.at[0, 0], left).wait_send()

    @pl.when(me % 2 == 0)
    def _():
        remote(left1, left1, l1_s, l1_r.at[0, 0], to_hub).wait_send()

    @pl.when(me >= 2)
    def _():
        remote(right2, right2, r2_s, r2_r.at[0, 0], from_hub).wait_send()

    remote(core_in, core_in, a_s, a_r.at[0], core).wait_send()
    remote(half, x_in, b_s, b_r.at[0], xpeer).wait_send()
    remote(core_in, core_in, c_s, c_r.at[0], core).wait_send()


def local_line(factors, eps_occ, eps_vir, tile_index, pair_offset):
    aux_count = lax.axis_size("aux")
    rows, tile_width = factors.shape
    chunks = tile_width // WIDTH
    f32, half = jnp.float32, jnp.bfloat16
    block = pltpu.VMEM((chunks, rows, WIDTH), f32)
    share = pltpu.VMEM((chunks, WIDTH // 2, tile_width), f32)
    dma = pltpu.SemaphoreType.DMA
    anywhere = pl.BlockSpec(memory_space=pl.ANY)
    pieces = [dma, dma((chunks, PARTS))]
    items = [dma, dma((chunks,))]
    pinned = [pltpu.with_memory_space_constraint(x, pltpu.HBM) for x in (factors, eps_occ, eps_vir)]
    return pl.pallas_call(
        functools.partial(line_kernel, aux_count),
        out_shape=pltpu.VMEM((rows, tile_width), f32),
        in_specs=[anywhere] * 5,
        out_specs=pl.BlockSpec(memory_space=pltpu.VMEM),
        scratch_shapes=[pltpu.VMEM((rows, tile_width), f32)]
        + [block] * 7
        + [pltpu.VMEM((rows, tile_width), half)] * 2
        + [pltpu.VMEM((chunks, rows, WIDTH), half)] * 2
        + [pltpu.VMEM((chunks, WIDTH, tile_width), f32), share, share, share]
        + [pltpu.VMEM((chunks, WIDTH, tile_width), f32)]
        + [pltpu.VMEM((WIDTH, tile_width), half)] * 2
        + [pltpu.VMEM((16, WIDTH), f32), pltpu.VMEM((1, tile_width), f32), pltpu.VMEM((chunks, WIDTH, WIDTH), f32)]
        + [pltpu.SMEM(eps_occ.shape, f32), pltpu.SMEM(eps_vir.shape, f32)]
        + [pltpu.SMEM((1,), jnp.int32)] * 2
        + pieces * 4
        + items * 3
        + [dma((PARTS,)), dma((4,))],
        compiler_params=pltpu.CompilerParams(
            collective_id=0, has_side_effects=True, vmem_limit_bytes=50 * 1024 * 1024
        ),
        name="pair_line",
    )(*pinned, tile_index, pair_offset)


def solution(mesh):
    in_specs = (P(("grp", "aux"), "occ"), P("grp"), P("grp"), P("grp"), P("grp"))
    out_specs = P(("grp", "aux"), "occ")
    body = local_line if mesh.shape["occ"] == LINE and mesh.shape["aux"] == SHARDS else local_ring
    return jax.shard_map(body, mesh=mesh, in_specs=in_specs, out_specs=out_specs, check_vma=False)
```
